32 devices in a mesh: groups: 2 (over y), ctx: 4 (over z), exp: 4 (over x, core), rep: 1.
Axes of the slice: x: 2, y: 2, z: 4, core: 2. Of those that a mesh axis runs over, the one named last changes fastest.
Arguments:
- queries: bfloat16 [2, 256, 4096], P('groups', 'ctx', ('exp', 'rep')), parts along dimension 0, may hold values from -16.25 to 16.25
- pages: bfloat16 [2, 2304, 2, 512], P('groups', 'ctx', None, 'exp'), parts along dimension 0, may hold values from -5.2 to 5.2
- cached_lengths: int32 [2, 4], P('groups'), parts along dimension 0, may hold values from 128 to 512
- residual_in: bfloat16 [2, 256, 2048], P('groups', ('ctx', 'exp')), parts along dimension 0, may hold values from -2.390625 to 2.390625
- out_weight: bfloat16 [4096, 2048], P(('exp', 'rep')), may hold values from -0.09375 to 0.09375
- norm_gain: float32 [2048], replicated, may hold values from 0.1 to 1.9
- expert_ids: int32 [2, 256, 8], P('groups', ('ctx', 'exp')), parts along dimension 0, may hold values from 0 to 15, all different within a row; in each aligned block of 16 rows (0 to 15, 16 to 31, ..., all dimensions but the last counted through in order) at most 8 rows name the same one
- route_scores: float32 [2, 256, 8], P('groups', ('ctx', 'exp')), parts along dimension 0, may hold values from 0.05 to 1
- expert_input: bfloat16 [16, 2048, 2, 384], P(('ctx', 'exp'), None, None, 'rep'), may hold values from -0.125 to 0.125
- expert_output: bfloat16 [16, 384, 2048], P(('ctx', 'exp'), 'rep'), may hold values from -0.3125 to 0.3125
Outputs:
- context: bfloat16 [2, 256, 4096], P('groups', 'ctx', ('exp', 'rep')), parts along dimension 0
- layer_out: bfloat16 [2, 256, 2048], P('groups', ('ctx', 'exp', 'rep')), parts along dimension 0
The draws below stay inside these ranges and needn't reach their ends.
There are 2 independent parts, one for each index of `groups`. The reference program is written for one: setup_inputs(seed, part) draws one part's arguments, and reference() takes and returns one part's arrays. A program takes and returns all parts, laid end to end along the dimension named above; an argument that names none is the same for every part. Nothing has to cross between parts.
Inputs may be any that keep to these rules, and one draw needn't show every extreme that they name: `expert_ids`: in every aligned block of 16 positions of one request, no expert is named by more than 8 of the block's rows, and in some blocks one expert by exactly 8; the 8 experts of a row differ.
All inputs are finite; a program needn't handle non-finite values.
Results may differ from the reference program's by a relative error of at most 0.015.
Values may be sent and summed in bfloat16 or wider, within the bound.
A program may use at most 128 MiB of HBM per device.

```python
import math
import jax
import jax.numpy as jnp
import numpy as np
from jax import lax

D = 2048
HEADS = 32
KV_HEADS = 4
HEAD = 128
TOPK = 8
EXPERT_FF = 384
REQS = 1
FRESH_DEV = 64
SLAB = 512
FRESH = 256
PAGE = 576
PAGE_COUNT = 4
PAGES_LEN = 2304
EXPERTS = 16
TOK_BLK = 16
MOST = 8
SPLITS = 1


def draw_queries(key, part):
    values = 2.0 * jax.random.normal(jax.random.fold_in(key, 11), (REQS, FRESH, HEADS * HEAD), jnp.float32)
    values = jnp.clip(values, -8.0, 8.0)
    return values.astype(jnp.bfloat16)


def draw_pages(key, part):
    values = 1.3 * jax.random.normal(jax.random.fold_in(key, 12), (REQS, PAGES_LEN, 2, KV_HEADS * HEAD), jnp.float32)
    values = jnp.clip(values, -5.2, 5.2)
    return values.astype(jnp.bfloat16)


def draw_cached_lengths(key, part):
    slab_count = PAGES_LEN // PAGE
    lowest = max(2, SLAB // 4)
    drawn_lengths = jax.random.randint(jax.random.fold_in(key, 13), (REQS, slab_count), lowest, SLAB + 1)
    full_pick = jax.random.randint(jax.random.fold_in(key, 14), (REQS, 1), 0, slab_count)
    filled = jnp.where(jnp.arange(slab_count, dtype=jnp.int32)[None, :] == full_pick, SLAB, drawn_lengths)
    return filled.astype(jnp.int32)


def level_of(stream_key, shape, pieces, least, top_value):
    loudness, own = 1.0, jax.random.fold_in(stream_key, 6)
    for position, parts in pieces:
        steps = jnp.exp(jax.random.uniform(jax.random.fold_in(own, position), (parts,), jnp.float32, least / len(pieces), top_value / len(pieces)))
        loudness = loudness * jnp.repeat(steps, shape[position] // parts).reshape([-1 if axis == position else 1 for axis in range(len(shape))])
    return loudness


def routed_block(rng, own, number, rows, count, top, bound, lean):
    ranking = jax.random.permutation(rng, count)
    heavy_load, ordinary = shares(count, rows * top, bound, lean, True), shares(count, rows * top, bound, lean, False)
    places = jnp.arange(count)

    def named(tallies, turn):
        used = int((tallies > 0).sum())
        fixed = max(1, used // 4)
        shifted = fixed + (places - fixed + turn * (used - fixed)) % max(1, count - fixed)
        return jnp.zeros((count,), jnp.int32).at[ranking[jnp.where(places < fixed, places, shifted)]].set(jnp.asarray(tallies, jnp.int32))

    tallies = jnp.where(number % 4 == 0, named(heavy_load, number // 4), named(ordinary, number - number // 4 - 1))
    mixed = jax.random.permutation(jax.random.fold_in(own, 3), count)
    donor, taker = mixed[0:count // 2 * 2:2], mixed[1:count // 2 * 2:2]
    room = jnp.minimum(tallies[donor] - 1, bound - tallies[taker]) // 2
    room = jnp.where((donor == ranking[0]) | (taker == ranking[0]) | (tallies[taker] == 0), 0, jnp.maximum(room, 0))
    shifted = jax.random.randint(jax.random.fold_in(own, 4), (count // 2,), 0, 1 << 20) % (room + 1)
    tallies = tallies.at[donor].add(-shifted).at[taker].add(shifted)
    labels = jnp.searchsorted(jnp.cumsum(tallies), jnp.arange(rows * top), side="right").astype(jnp.int32)
    listing = labels.reshape(top, rows).T
    listing = listing[jax.random.permutation(jax.random.fold_in(own, 1), rows)]
    turn = jax.random.randint(jax.random.fold_in(own, 2), (rows, 1), 0, top)
    return jnp.take_along_axis(listing, (jnp.arange(top)[None, :] + turn) % top, axis=1)


def shares(number_of, total, reach, skew, full):
    weights = [(1 << 20) // math.isqrt(standing ** skew) + 1 for standing in range(1, number_of + 1)]
    largest = reach if full else min(reach, max(-(-total // number_of), total * weights[0] // sum(weights)))
    least = 1 if total - largest >= number_of - 1 else 0
    given, surplus = [largest] + [least] * (number_of - 1), total - largest - least * (number_of - 1)
    while surplus > 0:
        free = [i for i in range(1, number_of) if given[i] < largest] or [i for i in range(1, number_of) if given[i] < reach]
        pool, left = sum([weights[i] for i in free]), surplus
        for i in free:
            more = min(reach - given[i], max(1, left * weights[i] // pool), surplus)
            given[i] = given[i] + more
            surplus = surplus - more
    return np.array(given)


def bell_draw(rng, dims, scale, limit, pieces=(), kind=jnp.bfloat16):
    drawn = jax.random.normal(rng, dims, jnp.float32) * scale
    if len(pieces) > 0:
        drawn = level_of(rng, dims, pieces, -0.22, 0.18) * drawn
    return jnp.clip(drawn, min=-limit, max=limit).astype(kind)


def setup_inputs(seed: int = 0, part: int = 0) -> dict:
    key_list = jax.random.split(jax.random.key(seed), 11)
    own_keys = jax.random.split(jax.random.fold_in(key_list[10], part), 11)
    queries = draw_queries(jax.random.fold_in(jax.random.fold_in(key_list[10], part), 71), part)
    pages = draw_pages(jax.random.fold_in(jax.random.fold_in(key_list[10], part), 71), part)
    cached_lengths = draw_cached_lengths(jax.random.fold_in(jax.random.fold_in(key_list[10], part), 71), part)
    residual_in = bell_draw(own_keys[3], (REQS, FRESH, D), 0.4, 2.390625, ((1, 16),))
    out_weight = bell_draw(key_list[4], (HEADS * HEAD, D), (HEADS * HEAD) ** -0.5, 0.09375, ((0, 4),))
    norm_gain = jnp.clip(1.0 + 0.18 * jax.random.normal(key_list[5], (D,), jnp.float32), 0.1, 1.9)
    expert_ids_keys = jax.random.split(jax.random.fold_in(own_keys[6], 1), REQS * FRESH // TOK_BLK)
    expert_ids_turns = jax.random.permutation(jax.random.fold_in(own_keys[6], 3), REQS * FRESH // TOK_BLK)
    expert_ids = jax.vmap(lambda own, number: routed_block(jax.random.fold_in(own_keys[6], 2), own, number, TOK_BLK, EXPERTS, TOPK, MOST, 2))(expert_ids_keys, expert_ids_turns).reshape((REQS, FRESH, TOPK))
    route_scores = jnp.clip(jnp.exp(math.log(1.0) - 2.9957323 * jax.random.uniform(own_keys[7], (REQS, FRESH, TOPK), jnp.float32) ** level_of(own_keys[7], (REQS, FRESH, TOPK), ((1, 16),), -0.2, 0.2)), 0.05, 1.0)
    expert_input = bell_draw(key_list[8], (EXPERTS, D, 2, EXPERT_FF), D ** -0.5, 0.125, ((0, 16),))
    expert_output = bell_draw(key_list[9], (EXPERTS, EXPERT_FF, D), EXPERT_FF ** -0.5, 0.3125, ((0, 16),))
    return dict(queries=queries, pages=pages, cached_lengths=cached_lengths, residual_in=residual_in, out_weight=out_weight, norm_gain=norm_gain, expert_ids=expert_ids, route_scores=route_scores, expert_input=expert_input, expert_output=expert_output)


floor_value = -1e+30
norm_epsilon = 1e-06

def normalize(hidden, norm_gain):
    widened = hidden.astype(jnp.float32)
    mean_square = lax.optimization_barrier(jnp.mean(widened * widened, axis=-1, keepdims=True))
    return (widened * lax.rsqrt(mean_square + norm_epsilon) * norm_gain).astype(jnp.bfloat16)

def expert_apply(normed_rows, weight_in, weight_out):
    inner_rows = jnp.einsum('nd,dgh->ngh', normed_rows.astype(jnp.float32), weight_in.astype(jnp.float32))
    activated = (jax.nn.silu(inner_rows[:, 0]) * inner_rows[:, 1]).astype(jnp.bfloat16)
    part_width = EXPERT_FF // SPLITS
    result = jnp.zeros((normed_rows.shape[0], D), jnp.float32)
    for portion in range(SPLITS):
        lower = portion * part_width
        partial_value = jnp.dot(activated[:, lower:lower + part_width], weight_out[lower:lower + part_width], preferred_element_type=jnp.float32)
        rounded_part = lax.optimization_barrier(partial_value.astype(jnp.bfloat16))
        result = result + rounded_part.astype(jnp.float32)
    return result

def reference(queries, pages, cached_lengths, residual_in, out_weight, norm_gain, expert_ids, route_scores, expert_input, expert_output):
    group_size = HEADS // KV_HEADS
    scaling = HEAD ** (-0.5)
    zero_index = jnp.int32(0)
    row_index = jnp.arange(PAGES_LEN, dtype=jnp.int32)
    page_number = row_index // PAGE
    offset = row_index - page_number * PAGE
    query_positions = jnp.arange(FRESH, dtype=jnp.int32)

    def one_head(flat_index):
        flat_index = flat_index.astype(jnp.int32)
        request = (flat_index // HEADS).astype(jnp.int32)
        head_number = (flat_index - request * HEADS).astype(jnp.int32)
        pair_head = (head_number // group_size).astype(jnp.int32)
        query_rows = lax.dynamic_slice(queries, (request, zero_index, (head_number * HEAD).astype(jnp.int32)), (1, FRESH, HEAD))[0]
        page_rows = lax.dynamic_slice(pages, (request, zero_index, zero_index, (pair_head * HEAD).astype(jnp.int32)), (1, PAGES_LEN, 2, HEAD))[0]
        lengths_row = lax.dynamic_slice(cached_lengths, (request, zero_index), (1, PAGE_COUNT))[0]
        live_length = lengths_row[page_number]
        in_cache = (offset < SLAB) & (offset < live_length)
        fresh_position = page_number * FRESH_DEV + offset - SLAB
        in_fresh = (offset >= SLAB)[None, :] & (fresh_position[None, :] <= query_positions[:, None])
        allowed = in_cache[None, :] | in_fresh
        scores = jnp.dot(query_rows, page_rows[:, 0].T, preferred_element_type=jnp.float32) * scaling
        masked = jnp.where(allowed, scores, floor_value)
        peaks = lax.optimization_barrier(jnp.max(masked, axis=1, keepdims=True))
        weights = jnp.where(allowed, jnp.exp(masked - peaks), 0.0)
        totals = lax.optimization_barrier(jnp.sum(weights, axis=1, keepdims=True))
        summed = jnp.dot(weights.astype(jnp.bfloat16), page_rows[:, 1], preferred_element_type=jnp.float32)
        return (summed / totals).astype(jnp.bfloat16)
    heads_out = lax.map(one_head, jnp.arange(REQS * HEADS, dtype=jnp.int32))
    context = heads_out.reshape(REQS, HEADS, FRESH, HEAD).transpose(0, 2, 1, 3).reshape(REQS, FRESH, HEADS * HEAD)
    projected = jnp.dot(context.reshape(REQS * FRESH, HEADS * HEAD), out_weight, preferred_element_type=jnp.float32).reshape(REQS, FRESH, D)
    hidden = (residual_in.astype(jnp.float32) + projected).astype(jnp.bfloat16)
    normed = normalize(hidden, norm_gain)
    token_count = REQS * FRESH
    flat_normed = normed.reshape(token_count, D)
    flat_ids = expert_ids.reshape(-1).astype(jnp.int32)
    combine = (route_scores / lax.optimization_barrier(jnp.sum(route_scores, axis=2, keepdims=True))).astype(jnp.bfloat16)
    combine = lax.optimization_barrier(combine).astype(jnp.float32).reshape(-1)
    sorted_rows = jnp.argsort(flat_ids, stable=True).astype(jnp.int32)
    counts = lax.optimization_barrier(jnp.sum((flat_ids[:, None] == jnp.arange(EXPERTS, dtype=jnp.int32)[None, :]).astype(jnp.int32), axis=0))
    starts = (jnp.cumsum(counts) - counts).astype(jnp.int32)
    row_limit = min(token_count * TOPK, token_count // TOK_BLK * MOST)
    padded = jnp.concatenate([sorted_rows, jnp.zeros((row_limit,), jnp.int32)])

    def add_expert(expert, mixture):
        picked = lax.dynamic_slice(padded, (starts[expert].astype(jnp.int32),), (row_limit,))
        alive_rows = jnp.arange(row_limit, dtype=jnp.int32) < counts[expert]
        tokens = picked // TOPK
        outputs = expert_apply(flat_normed[tokens], expert_input[expert], expert_output[expert])
        scaled = outputs * jnp.where(alive_rows, combine[picked], 0.0)[:, None]
        return mixture.at[tokens].add(scaled)
    mixture = lax.fori_loop(0, EXPERTS, add_expert, jnp.zeros((token_count, D), jnp.float32))
    layer_out = (hidden.astype(jnp.float32).reshape(token_count, D) + mixture).astype(jnp.bfloat16).reshape(REQS, FRESH, D)
    return (context, layer_out)
```

```python
import functools

import jax
import jax.numpy as jnp
from jax import lax
from jax.experimental import pallas as pl
from jax.experimental.pallas import tpu as pltpu
from jax.sharding import PartitionSpec as P

HEAD = 128


floor_value = -1e30
norm_epsilon = 1e-06


def normalize(hidden, norm_gain):
    widened = hidden.astype(jnp.float32)
    mean_square = jnp.mean(widened * widened, axis=-1, keepdims=True)
    return (widened * lax.rsqrt(mean_square + norm_epsilon) * norm_gain).astype(jnp.bfloat16)


def attend_piece(query_rows, page_rows, allowed):
    scaling = query_rows.shape[-1] ** (-0.5)
    scores = (
        jnp.einsum(
            "rqhe,rke->rqhk", query_rows, page_rows[:, :, 0], preferred_element_type=jnp.float32
        )
        * scaling
    )
    permitted = allowed[:, :, None, :]
    masked = jnp.where(permitted, scores, floor_value)
    peaks = jnp.max(masked, axis=-1)
    weights = jnp.where(permitted, jnp.exp(masked - peaks[..., None]), 0.0)
    totals = jnp.sum(weights, axis=-1)
    summed = jnp.einsum(
        "rqhk,rke->rqhe",
        weights.astype(jnp.bfloat16),
        page_rows[:, :, 1],
        preferred_element_type=jnp.float32,
    )
    return (peaks, totals, summed)


def merge_partials(earlier, later):
    peaks = jnp.maximum(earlier[0], later[0])
    later_scale = jnp.exp(later[0] - peaks)
    totals = later[1] * later_scale
    summed = later[2] * later_scale[..., None]
    return (peaks, totals, summed)


def rows_mask(row_index, lengths, query_positions, slab_size, fresh_block):
    page_size = slab_size + fresh_block
    page_number = row_index // page_size
    offset = row_index - page_number * page_size
    page_count = lengths.shape[1]
    picker = page_number[None, :] == jnp.arange(page_count, dtype=jnp.int32)[:, None]
    live_length = jnp.sum(jnp.where(picker[None], lengths[:, :, None], 0), axis=1)
    in_cache = (offset < slab_size)[None, :] & (offset[None, :] < live_length)
    fresh_position = page_number * fresh_block + offset - slab_size
    in_fresh = (offset >= slab_size)[None, :] & (
        fresh_position[None, :] <= query_positions[:, None]
    )
    return in_cache[:, None, :] | in_fresh[None, :, :]


def per_device(
    queries,
    pages,
    cached_lengths,
    residual_in,
    out_weight,
    norm_gain,
    expert_ids,
    route_scores,
    expert_input,
    expert_output,
):
    requests, fresh_block, query_width = queries.shape
    local_heads = query_width // HEAD
    core_place = lax.axis_index("rep")
    page_place = lax.axis_index("ctx")
    rep_count = lax.axis_size("rep")
    page_size = pages.shape[1]
    slab_size = page_size - fresh_block
    own_positions = page_place * fresh_block + jnp.arange(fresh_block, dtype=jnp.int32)
    query_rows = queries.reshape(requests, fresh_block, local_heads, HEAD)
    start_state = (
        jnp.full((requests, fresh_block, local_heads), floor_value, jnp.float32),
        jnp.zeros((requests, fresh_block, local_heads), jnp.float32),
        jnp.zeros((requests, fresh_block, local_heads, HEAD), jnp.float32),
    )
    page_piece = lax.all_gather(pages, "ctx", axis=1, tiled=True)
    row_index = jnp.arange(page_piece.shape[1], dtype=jnp.int32)
    allowed = rows_mask(row_index, cached_lengths, own_positions, slab_size, fresh_block)
    peaks, totals, summed = merge_partials(
        start_state, attend_piece(query_rows, page_piece, allowed)
    )
    context = (
        (summed / totals[..., None])
        .astype(jnp.bfloat16)
        .reshape(requests, fresh_block, query_width)
    )
    projected = jnp.dot(
        context.reshape(requests * fresh_block, query_width),
        out_weight,
        preferred_element_type=jnp.float32,
    ).reshape(requests, fresh_block, -1)
    token_block = residual_in.shape[1]
    share_size = token_block // rep_count
    own_share = lax.psum_scatter(
        projected.astype(jnp.bfloat16), ("exp", "rep"), scatter_dimension=1, tiled=True
    ).astype(jnp.float32)
    own_residual = lax.dynamic_slice_in_dim(residual_in, core_place * share_size, share_size, 1)
    own_hidden = (own_residual.astype(jnp.float32) + own_share).astype(jnp.bfloat16)
    normed = lax.all_gather(normalize(own_hidden, norm_gain), "rep", axis=1, tiled=True)
    top_count = expert_ids.shape[2]
    expert_count = lax.axis_size("ctx") * lax.axis_size("exp")
    most_rows = max(2, (token_block * top_count + expert_count - 1) // expert_count)
    capacity = requests * most_rows
    model_width = normed.shape[2]
    token_count = requests * token_block
    flat_ids = expert_ids.reshape(-1)
    row_count = flat_ids.shape[0]
    chosen = (flat_ids[:, None] == jnp.arange(expert_count, dtype=jnp.int32)[None, :]).astype(
        jnp.int32
    )
    earlier_rows = jnp.cumsum(chosen, axis=0) - chosen
    slot_rank = jnp.sum(earlier_rows * chosen, axis=1)
    slot_index = flat_ids * capacity + slot_rank
    slot_onehot = (
        slot_index[:, None] == jnp.arange(expert_count * capacity, dtype=jnp.int32)[None, :]
    ).astype(jnp.bfloat16)
    token_onehot = (
        (jnp.arange(row_count, dtype=jnp.int32) // top_count)[:, None]
        == jnp.arange(token_count, dtype=jnp.int32)[None, :]
    ).astype(jnp.bfloat16)
    placement = jnp.dot(slot_onehot.T, token_onehot, preferred_element_type=jnp.float32).astype(
        jnp.bfloat16
    )
    outgoing = jnp.dot(
        placement, normed.reshape(token_count, model_width), preferred_element_type=jnp.float32
    )
    outgoing = outgoing.astype(jnp.bfloat16).reshape(expert_count, capacity, model_width)
    scores_sum = jnp.sum(route_scores, axis=2, keepdims=True)
    combine = (route_scores / scores_sum).astype(jnp.bfloat16).reshape(-1)
    gathering = jnp.dot(
        (token_onehot * combine[:, None]).T, slot_onehot, preferred_element_type=jnp.float32
    ).astype(jnp.bfloat16)
    gate_up = expert_input[0]
    down_weight = expert_output[0]
    arrived_rows = lax.all_to_all(outgoing, ("ctx", "exp"), split_axis=0, concat_axis=0, tiled=True)
    inner_rows = jnp.einsum(
        "nd,dgh->ngh",
        arrived_rows.reshape(-1, model_width),
        gate_up,
        preferred_element_type=jnp.float32,
    )
    activated = (jax.nn.silu(inner_rows[:, 0]) * inner_rows[:, 1]).astype(jnp.bfloat16)
    result = jnp.dot(activated, down_weight, preferred_element_type=jnp.float32).astype(
        jnp.bfloat16
    )
    returned = lax.all_to_all(
        result.reshape(arrived_rows.shape), ("ctx", "exp"), split_axis=0, concat_axis=0, tiled=True
    )
    mixture = jnp.dot(
        gathering,
        returned.reshape(expert_count * capacity, model_width),
        preferred_element_type=jnp.float32,
    )
    own_mixture = lax.psum_scatter(
        mixture.reshape(requests, token_block, model_width).astype(jnp.bfloat16),
        "rep",
        scatter_dimension=1,
        tiled=True,
    ).astype(jnp.float32)
    layer_out = (own_hidden.astype(jnp.float32) + own_mixture).astype(jnp.bfloat16)
    return (context, layer_out)


BF = jnp.bfloat16
F32 = jnp.float32
MESH = pl.DeviceIdType.MESH
VMEM_LIMIT = 60 * 1024 * 1024


def fused_kernel(
    ctx_count, exp_count, capacity,
    lengths, query, page, residual, gain, ids, scores, w_out, w_in, w_down,
    context_out, layer_out,
    kv, q_rows, bias, peak, total, accum, wo, wi, wg, wu, wd,
    ids_all, scores_all, combine_all, place, gather,
    rs_full, rs_send, rs_recv, hidden, nz, x_send, x_recv, x_rows, y_send, y_recv, y_rows, mix_send, mix_recv,
    kv_left, kv_right, kv_recv, w_sem,
    ids_s, ids_r, sc_s, sc_r, rs_s, rs_r, nz_s, nz_r, dx_s, dx_r, ret_s, ret_r, mix_s, mix_r,
):
    ci = lax.axis_index("ctx")
    ei = lax.axis_index("exp")
    fresh = query.shape[0]
    heads = query.shape[1] // HEAD
    page_size = page.shape[0]
    slab = page_size - fresh
    rows = residual.shape[0]
    width = residual.shape[1]
    top = ids.shape[1]
    scaling = HEAD ** (-0.5) * 1.4426950408889634

    def ctx_peer(k):
        return {"ctx": lax.rem(ci + k, ctx_count)}

    def exp_peer(k):
        return {"exp": lax.rem(ei + k, exp_count)}

    def remote(src, dst, ss, rs, where):
        return pltpu.make_async_remote_copy(
            src_ref=src, dst_ref=dst, send_sem=ss, recv_sem=rs, device_id=where, device_id_type=MESH
        )

    copies_w = [
        pltpu.make_async_copy(w_out, wo, w_sem.at[0]),
        pltpu.make_async_copy(w_in, wi, w_sem.at[1]),
        pltpu.make_async_copy(w_down, wd, w_sem.at[2]),
    ]

    barrier = pltpu.get_barrier_semaphore()
    for k in range(1, ctx_count):
        pl.semaphore_signal(barrier, inc=1, device_id=ctx_peer(k), device_id_type=MESH)
    for k in range(1, exp_count):
        pl.semaphore_signal(barrier, inc=1, device_id=exp_peer(k), device_id_type=MESH)
    pl.semaphore_wait(barrier, ctx_count + exp_count - 2)

    def right_copy(src, p):
        return remote(src, kv.at[p], kv_right.at[p], kv_recv.at[p], {"ctx": ci + 1})

    def left_copy(src, p):
        return remote(src, kv.at[p], kv_left.at[p], kv_recv.at[p], {"ctx": ci - 1})

    @pl.when(ci < ctx_count - 1)
    def _():
        right_copy(page, ci).start()

    @pl.when(ci > 0)
    def _():
        left_copy(page, ci).start()

    small = []
    for k in range(1, ctx_count):
        small.append(remote(ids, ids_all.at[k], ids_s.at[k], ids_r.at[k], ctx_peer(k)))
        small.append(remote(scores, scores_all.at[k], sc_s.at[k], sc_r.at[k], ctx_peer(k)))
    for c in small:
        c.start()
    for c in copies_w:
        c.start()

    for h in range(heads):
        q_rows[h * fresh:(h + 1) * fresh, :] = query[:, h * HEAD:(h + 1) * HEAD]
    accum[...] = jnp.zeros_like(accum)
    total[...] = jnp.zeros_like(total)
    peak[...] = jnp.full_like(peak, floor_value)

    offset = lax.broadcasted_iota(jnp.int32, (fresh, page_size), 1)
    position = lax.broadcasted_iota(jnp.int32, (fresh, page_size), 0) + ci * fresh

    def attend(source, p):
        live = lengths[p]
        cached = (offset < slab) & (offset < live)
        new = (offset >= slab) & (p * fresh + offset - slab <= position)
        bias[...] = jnp.where(cached | new, 0.0, floor_value)
        both = source[...]
        keys = both[:, 0, :]
        values = both[:, 1, :]
        step = 2 if heads % 2 == 0 else 1
        for h in range(0, heads, step):
            sl = slice(h * fresh, (h + step) * fresh)
            s = lax.dot_general(
                q_rows[sl, :], keys, (((1,), (1,)), ((), ())), preferred_element_type=F32
            )
            s = jnp.concatenate([s[i * fresh:(i + 1) * fresh] + bias[...] for i in range(step)], 0)
            old = peak[sl, :]
            now = jnp.maximum(old, jnp.max(s, axis=1, keepdims=True))
            w = jnp.exp2((s - now[:, :1]) * scaling)
            fade = jnp.exp2((old - now) * scaling)
            total[sl, :] = total[sl, :] * fade + jnp.sum(w, axis=1, keepdims=True)
            accum[sl, :] = accum[sl, :] * fade + jnp.dot(
                w.astype(BF), values, preferred_element_type=F32
            )
            peak[sl, :] = now

    attend(page, ci)

    copies_w[1].wait()
    depth = 256

    def unpack(i, carry):
        at = pl.ds(pl.multiple_of(i * depth, depth), depth)
        block = wi[at]
        wg[at, :] = block[:, 0, :]
        wu[at, :] = block[:, 1, :]
        return carry

    lax.fori_loop(0, width // depth, unpack, 0)

    combined = scores[...] / jnp.sum(scores[...], axis=1, keepdims=True)
    ids_all[0] = ids[...]
    combine_all[0] = combined.astype(BF).astype(F32)
    for c in small:
        c.wait()
    for k in range(1, ctx_count):
        given = scores_all[k]
        combine_all[k] = (given / jnp.sum(given, axis=1, keepdims=True)).astype(BF).astype(F32)

    lanes = exp_count * capacity
    lane = lax.broadcasted_iota(jnp.int32, (rows, lanes), 1)
    wanted = ci * exp_count + lax.rem(ei + lane // capacity, exp_count)
    seat = (lane - lane // capacity * capacity).astype(F32)
    earlier = (
        lax.broadcasted_iota(jnp.int32, (rows, rows), 1)
        < lax.broadcasted_iota(jnp.int32, (rows, rows), 0)
    ).astype(F32)
    for k in range(ctx_count):
        chosen = jnp.zeros((rows, lanes), F32)
        portion = jnp.zeros((rows, lanes), F32)
        for j in range(top):
            hit = ids_all[k, :, j:j + 1] == wanted
            chosen = jnp.where(hit, 1.0, chosen)
            portion = jnp.where(hit, combine_all[k, :, j:j + 1], portion)
        rank = jnp.dot(earlier.astype(BF), chosen.astype(BF), preferred_element_type=F32)
        seated = (chosen > 0.5) & (rank == seat)
        place[k] = jnp.where(seated, 1.0, 0.0)
        gather[k] = jnp.where(seated, portion, 0.0)

    def arrival(i, carry):
        d = i // 2 + 1
        p = jnp.where(lax.rem(i, 2) == 0, ci - d, ci + d)

        @pl.when((p >= 0) & (p < ctx_count))
        def _():
            right_copy(kv.at[p], p).wait_recv()

            @pl.when((p < ci) & (ci < ctx_count - 1))
            def _():
                right_copy(kv.at[p], p).start()

            @pl.when((p > ci) & (ci > 0))
            def _():
                left_copy(kv.at[p], p).start()

            attend(kv.at[p], p)

        return carry

    lax.fori_loop(0, 2 * (ctx_count - 1), arrival, 0)

    for h in range(heads):
        sl = slice(h * fresh, (h + 1) * fresh)
        context_out[:, h * HEAD:(h + 1) * HEAD] = (accum[sl, :] / total[sl, :]).astype(BF)

    copies_w[0].wait()

    pieces = 4
    piece = width // pieces
    own_share = []
    rs_copies = []
    for n in range(pieces):
        cols = slice(n * piece, (n + 1) * piece)
        part = jnp.dot(context_out[...], wo[:, cols], preferred_element_type=F32)
        rs_full[n] = part
        for k in range(1, exp_count):
            at = pl.ds(pl.multiple_of(lax.rem(ei + k, exp_count) * rows, rows), rows)
            rs_send[k, n] = rs_full[n, at, :].astype(BF)
            c = remote(rs_send.at[k, n], rs_recv.at[k, n], rs_s.at[k, n], rs_r.at[k, n], exp_peer(k))
            c.start()
            rs_copies.append(c)
    mine = pl.ds(pl.multiple_of(ei * rows, rows), rows)
    square = jnp.zeros((rows, 1), F32)
    for n in range(pieces):
        cols = slice(n * piece, (n + 1) * piece)
        share = rs_full[n, mine, :]
        for k in range(1, exp_count):
            rs_copies[n * (exp_count - 1) + k - 1].wait_recv()
            share = share + rs_recv[k, n].astype(F32)
        h = (residual[:, cols].astype(F32) + share).astype(BF)
        hidden[:, cols] = h
        wide = h.astype(F32)
        square = square + jnp.sum(wide * wide, axis=1, keepdims=True)
    inverse = lax.rsqrt(square / width + norm_epsilon)
    nz[0] = (hidden[...].astype(F32) * inverse * gain[...]).astype(BF)

    nz_copies = {}
    order = [1, ctx_count - 1] + list(range(2, ctx_count - 1)) if ctx_count > 2 else list(range(1, ctx_count))
    for k in reversed(order):
        c = remote(nz.at[0], nz.at[k], nz_s.at[k], nz_r.at[k], ctx_peer(k))
        c.start()
        nz_copies[k] = c

    dx_copies = []
    for k in [0] + order:
        if k:
            nz_copies[k].wait_recv()
        routed = lax.dot_general(
            place[k].astype(BF), nz[k], (((0,), (0,)), ((), ())), preferred_element_type=F32
        )
        for j in range(exp_count):
            block = routed[j * capacity:(j + 1) * capacity].astype(BF)
            if j == 0:
                x_recv[0, k] = block
            else:
                x_send[j, k] = block
                c = remote(x_send.at[j, k], x_recv.at[j, k], dx_s.at[j, k], dx_r.at[j, k], exp_peer(j))
                c.start()
                dx_copies.append(c)
    copies_w[2].wait()
    for c in dx_copies:
        c.wait_recv()
    for j in range(exp_count):
        for k in range(ctx_count):
            at = slice((j * ctx_count + k) * capacity, (j * ctx_count + k + 1) * capacity)
            x_rows[at, :] = x_recv[j, k].astype(F32)
    x = x_rows[...].astype(BF)
    gate = jnp.dot(x, wg[...], preferred_element_type=F32)
    up = jnp.dot(x, wu[...], preferred_element_type=F32)
    act = (gate / (1.0 + jnp.exp(-gate)) * up).astype(BF)
    span = ctx_count * capacity
    ret_copies = []
    result = jnp.dot(act, wd[...], preferred_element_type=F32)
    for j in range(exp_count):
        block = result[j * span:(j + 1) * span].astype(BF)
        if j == 0:
            y_recv[0] = block
        else:
            y_send[j] = block
            c = remote(y_send.at[j], y_recv.at[j], ret_s.at[j], ret_r.at[j], exp_peer(exp_count - j))
            c.start()
            ret_copies.append(c)
    for c in ret_copies:
        c.wait_recv()
    for j in range(exp_count):
        y_rows[j] = y_recv[j].astype(F32)
    mix_copies = []
    own = None
    for k in list(reversed(order)) + [0]:
        rows_k = jnp.concatenate(
            [y_rows[j, k * capacity:(k + 1) * capacity] for j in range(exp_count)], 0
        ).astype(BF)
        mixed = jnp.dot(gather[k].astype(BF), rows_k, preferred_element_type=F32)
        if k == 0:
            own = mixed
        else:
            mix_send[k] = mixed.astype(BF)
            c = remote(mix_send.at[k], mix_recv.at[k], mix_s.at[k], mix_r.at[k], ctx_peer(ctx_count - k))
            c.start()
            mix_copies.append(c)
    out = hidden[...].astype(F32) + own
    for c, k in zip(reversed(mix_copies), order):
        c.wait_recv()
        out = out + mix_recv[k].astype(F32)
    layer_out[...] = out.astype(BF)

    for c in rs_copies + list(nz_copies.values()) + dx_copies + ret_copies + mix_copies:
        c.wait_send()

    @pl.when(ci < ctx_count - 1)
    def _():
        right_copy(page, ci).wait_send()

    @pl.when(ci > 0)
    def _():
        left_copy(page, ci).wait_send()

    def drain(p, carry):
        @pl.when((p < ci) & (ci < ctx_count - 1))
        def _():
            right_copy(kv.at[p], p).wait_send()

        @pl.when((p > ci) & (ci > 0))
        def _():
            left_copy(kv.at[p], p).wait_send()

        return carry

    lax.fori_loop(0, ctx_count, drain, 0)


def fused_device(
    ctx_count, exp_count, queries, pages, cached_lengths, residual_in, out_weight, norm_gain,
    expert_ids, route_scores, expert_input, expert_output,
):
    fresh, query_width = queries.shape[1:]
    page_size = pages.shape[1]
    rows, width = residual_in.shape[1:]
    top = expert_ids.shape[2]
    hidden_width = expert_input.shape[3]
    experts = ctx_count * exp_count
    capacity = max(2, -(-rows * top // experts))
    stacked = query_width // HEAD * fresh
    span = ctx_count * capacity
    vm = pl.BlockSpec(memory_space=pltpu.VMEM)
    sm = pl.BlockSpec(memory_space=pltpu.SMEM)
    hbm = pl.BlockSpec(memory_space=pl.ANY)
    dma = pltpu.SemaphoreType.DMA
    V = pltpu.VMEM
    lanes = exp_count * capacity
    pieces = 4
    context, layer_out = pl.pallas_call(
        functools.partial(fused_kernel, ctx_count, exp_count, capacity),
        out_shape=(
            jax.ShapeDtypeStruct((fresh, query_width), BF),
            jax.ShapeDtypeStruct((rows, width), BF),
        ),
        in_specs=[sm, vm, vm, vm, vm, vm, vm, hbm, hbm, hbm],
        out_specs=(vm, vm),
        scratch_shapes=[
            V((ctx_count,) + pages.shape[1:], BF),
            V((stacked, HEAD), BF),
            V((fresh, page_size), F32),
            V((stacked, HEAD), F32),
            V((stacked, HEAD), F32),
            V((stacked, HEAD), F32),
            V(out_weight.shape, BF),
            V(expert_input.shape[1:], BF),
            V((width, hidden_width), BF),
            V((width, hidden_width), BF),
            V(expert_output.shape[1:], BF),
            V((ctx_count, rows, top), jnp.int32),
            V((ctx_count, rows, top), F32),
            V((ctx_count, rows, top), F32),
            V((ctx_count, rows, lanes), F32),
            V((ctx_count, rows, lanes), F32),
            V((pieces, fresh, width // pieces), F32),
            V((exp_count, pieces, rows, width // pieces), BF),
            V((exp_count, pieces, rows, width // pieces), BF),
            V((rows, width), BF),
            V((ctx_count, rows, width), BF),
            V((exp_count, ctx_count, capacity, width), BF),
            V((exp_count, ctx_count, capacity, width), BF),
            V((exp_count * span, width), F32),
            V((exp_count, span, width), BF),
            V((exp_count, span, width), BF),
            V((exp_count, span, width), F32),
            V((ctx_count, rows, width), BF),
            V((ctx_count, rows, width), BF),
            dma((ctx_count,)), dma((ctx_count,)), dma((ctx_count,)), dma((3,)),
            dma((ctx_count,)), dma((ctx_count,)), dma((ctx_count,)), dma((ctx_count,)),
            dma((exp_count, pieces)), dma((exp_count, pieces)),
            dma((ctx_count,)), dma((ctx_count,)),
            dma((exp_count, ctx_count)), dma((exp_count, ctx_count)),
            dma((exp_count,)), dma((exp_count,)),
            dma((ctx_count,)), dma((ctx_count,)),
        ],
        compiler_params=pltpu.CompilerParams(
            collective_id=0, has_side_effects=True, vmem_limit_bytes=VMEM_LIMIT
        ),
    )(
        cached_lengths[0], queries[0], pages[0], residual_in[0], norm_gain.reshape(1, width),
        expert_ids[0], route_scores[0], out_weight, expert_input[0], expert_output[0],
    )
    return context[None], layer_out[None]


def fused_fits(mesh):
    return mesh.shape["rep"] == 1 and mesh.shape["ctx"] <= 8


def solution(mesh):
    in_specs = (
        P("groups", "ctx", ("exp", "rep")),
        P("groups", "ctx", None, "exp"),
        P("groups", None),
        P("groups", ("ctx", "exp"), None),
        P(("exp", "rep"), None),
        P(),
        P("groups", ("ctx", "exp"), None),
        P("groups", ("ctx", "exp"), None),
        P(("ctx", "exp"), None, None, "rep"),
        P(("ctx", "exp"), "rep", None),
    )
    out_specs = (P("groups", "ctx", ("exp", "rep")), P("groups", ("ctx", "exp", "rep"), None))
    body = per_device
    if fused_fits(mesh):
        body = functools.partial(fused_device, mesh.shape["ctx"], mesh.shape["exp"])
    return jax.shard_map(
        body, mesh=mesh, in_specs=in_specs, out_specs=out_specs, check_vma=False
    )
```

```python
import functools

import jax
import jax.numpy as jnp
from jax import lax
from jax.experimental import pallas as pl
from jax.experimental.pallas import tpu as pltpu
from jax.sharding import PartitionSpec as P

HEAD = 128


floor_value = -1e30
norm_epsilon = 1e-06


def normalize(hidden, norm_gain):
    widened = hidden.astype(jnp.float32)
    mean_square = jnp.mean(widened * widened, axis=-1, keepdims=True)
    return (widened * lax.rsqrt(mean_square + norm_epsilon) * norm_gain).astype(jnp.bfloat16)


def attend_piece(query_rows, page_rows, allowed):
    scaling = query_rows.shape[-1] ** (-0.5)
    scores = (
        jnp.einsum(
            "rqhe,rke->rqhk", query_rows, page_rows[:, :, 0], preferred_element_type=jnp.float32
        )
        * scaling
    )
    permitted = allowed[:, :, None, :]
    masked = jnp.where(permitted, scores, floor_value)
    peaks = jnp.max(masked, axis=-1)
    weights = jnp.where(permitted, jnp.exp(masked - peaks[..., None]), 0.0)
    totals = jnp.sum(weights, axis=-1)
    summed = jnp.einsum(
        "rqhk,rke->rqhe",
        weights.astype(jnp.bfloat16),
        page_rows[:, :, 1],
        preferred_element_type=jnp.float32,
    )
    return (peaks, totals, summed)


def merge_partials(earlier, later):
    peaks = jnp.maximum(earlier[0], later[0])
    later_scale = jnp.exp(later[0] - peaks)
    totals = later[1] * later_scale
    summed = later[2] * later_scale[..., None]
    return (peaks, totals, summed)


def rows_mask(row_index, lengths, query_positions, slab_size, fresh_block):
    page_size = slab_size + fresh_block
    page_number = row_index // page_size
    offset = row_index - page_number * page_size
    page_count = lengths.shape[1]
    picker = page_number[None, :] == jnp.arange(page_count, dtype=jnp.int32)[:, None]
    live_length = jnp.sum(jnp.where(picker[None], lengths[:, :, None], 0), axis=1)
    in_cache = (offset < slab_size)[None, :] & (offset[None, :] < live_length)
    fresh_position = page_number * fresh_block + offset - slab_size
    in_fresh = (offset >= slab_size)[None, :] & (
        fresh_position[None, :] <= query_positions[:, None]
    )
    return in_cache[:, None, :] | in_fresh[None, :, :]


def per_device(
    queries,
    pages,
    cached_lengths,
    residual_in,
    out_weight,
    norm_gain,
    expert_ids,
    route_scores,
    expert_input,
    expert_output,
):
    requests, fresh_block, query_width = queries.shape
    local_heads = query_width // HEAD
    core_place = lax.axis_index("rep")
    page_place = lax.axis_index("ctx")
    rep_count = lax.axis_size("rep")
    page_size = pages.shape[1]
    slab_size = page_size - fresh_block
    own_positions = page_place * fresh_block + jnp.arange(fresh_block, dtype=jnp.int32)
    query_rows = queries.reshape(requests, fresh_block, local_heads, HEAD)
    start_state = (
        jnp.full((requests, fresh_block, local_heads), floor_value, jnp.float32),
        jnp.zeros((requests, fresh_block, local_heads), jnp.float32),
        jnp.zeros((requests, fresh_block, local_heads, HEAD), jnp.float32),
    )
    page_piece = lax.all_gather(pages, "ctx", axis=1, tiled=True)
    row_index = jnp.arange(page_piece.shape[1], dtype=jnp.int32)
    allowed = rows_mask(row_index, cached_lengths, own_positions, slab_size, fresh_block)
    peaks, totals, summed = merge_partials(
        start_state, attend_piece(query_rows, page_piece, allowed)
    )
    context = (
        (summed / totals[..., None])
        .astype(jnp.bfloat16)
        .reshape(requests, fresh_block, query_width)
    )
    projected = jnp.dot(
        context.reshape(requests * fresh_block, query_width),
        out_weight,
        preferred_element_type=jnp.float32,
    ).reshape(requests, fresh_block, -1)
    token_block = residual_in.shape[1]
    share_size = token_block // rep_count
    own_share = lax.psum_scatter(
        projected.astype(jnp.bfloat16), ("exp", "rep"), scatter_dimension=1, tiled=True
    ).astype(jnp.float32)
    own_residual = lax.dynamic_slice_in_dim(residual_in, core_place * share_size, share_size, 1)
    own_hidden = (own_residual.astype(jnp.float32) + own_share).astype(jnp.bfloat16)
    normed = lax.all_gather(normalize(own_hidden, norm_gain), "rep", axis=1, tiled=True)
    top_count = expert_ids.shape[2]
    expert_count = lax.axis_size("ctx") * lax.axis_size("exp")
    most_rows = max(2, (token_block * top_count + expert_count - 1) // expert_count)
    capacity = requests * most_rows
    model_width = normed.shape[2]
    token_count = requests * token_block
    flat_ids = expert_ids.reshape(-1)
    row_count = flat_ids.shape[0]
    chosen = (flat_ids[:, None] == jnp.arange(expert_count, dtype=jnp.int32)[None, :]).astype(
        jnp.int32
    )
    earlier_rows = jnp.cumsum(chosen, axis=0) - chosen
    slot_rank = jnp.sum(earlier_rows * chosen, axis=1)
    slot_index = flat_ids * capacity + slot_rank
    slot_onehot = (
        slot_index[:, None] == jnp.arange(expert_count * capacity, dtype=jnp.int32)[None, :]
    ).astype(jnp.bfloat16)
    token_onehot = (
        (jnp.arange(row_count, dtype=jnp.int32) // top_count)[:, None]
        == jnp.arange(token_count, dtype=jnp.int32)[None, :]
    ).astype(jnp.bfloat16)
    placement = jnp.dot(slot_onehot.T, token_onehot, preferred_element_type=jnp.float32).astype(
        jnp.bfloat16
    )
    outgoing = jnp.dot(
        placement, normed.reshape(token_count, model_width), preferred_element_type=jnp.float32
    )
    outgoing = outgoing.astype(jnp.bfloat16).reshape(expert_count, capacity, model_width)
    scores_sum = jnp.sum(route_scores, axis=2, keepdims=True)
    combine = (route_scores / scores_sum).astype(jnp.bfloat16).reshape(-1)
    gathering = jnp.dot(
        (token_onehot * combine[:, None]).T, slot_onehot, preferred_element_type=jnp.float32
    ).astype(jnp.bfloat16)
    gate_up = expert_input[0]
    down_weight = expert_output[0]
    arrived_rows = lax.all_to_all(outgoing, ("ctx", "exp"), split_axis=0, concat_axis=0, tiled=True)
    inner_rows = jnp.einsum(
        "nd,dgh->ngh",
        arrived_rows.reshape(-1, model_width),
        gate_up,
        preferred_element_type=jnp.float32,
    )
    activated = (jax.nn.silu(inner_rows[:, 0]) * inner_rows[:, 1]).astype(jnp.bfloat16)
    result = jnp.dot(activated, down_weight, preferred_element_type=jnp.float32).astype(
        jnp.bfloat16
    )
    returned = lax.all_to_all(
        result.reshape(arrived_rows.shape), ("ctx", "exp"), split_axis=0, concat_axis=0, tiled=True
    )
    mixture = jnp.dot(
        gathering,
        returned.reshape(expert_count * capacity, model_width),
        preferred_element_type=jnp.float32,
    )
    own_mixture = lax.psum_scatter(
        mixture.reshape(requests, token_block, model_width).astype(jnp.bfloat16),
        "rep",
        scatter_dimension=1,
        tiled=True,
    ).astype(jnp.float32)
    layer_out = (own_hidden.astype(jnp.float32) + own_mixture).astype(jnp.bfloat16)
    return (context, layer_out)


BF = jnp.bfloat16
F32 = jnp.float32
MESH = pl.DeviceIdType.MESH
VMEM_LIMIT = 60 * 1024 * 1024


def fused_kernel(
    ctx_count, exp_count, capacity,
    lengths, query, page, residual, gain, ids, scores, w_out, w_in, w_down,
    context_out, layer_out,
    kv, q_rows, bias, peak, total, accum, wo, wi, wg, wu, wd,
    ids_all, scores_all, combine_all, place, gather,
    rs_full, rs_send, rs_recv, hidden, nz, x_send, x_recv, x_rows, y_send, y_recv, mix_send, mix_recv,
    kv_left, kv_right, kv_recv, w_sem,
    ids_s, ids_r, sc_s, sc_r, rs_s, rs_r, nz_s, nz_r, dx_s, dx_r, ret_s, ret_r, mix_s, mix_r,
):
    ci = lax.axis_index("ctx")
    ei = lax.axis_index("exp")
    fresh = query.shape[0]
    heads = query.shape[1] // HEAD
    page_size = page.shape[0]
    slab = page_size - fresh
    rows = residual.shape[0]
    width = residual.shape[1]
    top = ids.shape[0]
    chunks = kv.shape[1]
    chunk = kv.shape[2]
    scaling = HEAD ** (-0.5) * 1.4426950408889634

    def ctx_peer(k):
        return {"ctx": lax.rem(ci + k, ctx_count)}

    def exp_peer(k):
        return {"exp": lax.rem(ei + k, exp_count)}

    def remote(src, dst, ss, rs, where):
        return pltpu.make_async_remote_copy(
            src_ref=src, dst_ref=dst, send_sem=ss, recv_sem=rs, device_id=where, device_id_type=MESH
        )

    copies_w = [
        pltpu.make_async_copy(w_out, wo, w_sem.at[0]),
        pltpu.make_async_copy(w_in, wi, w_sem.at[1]),
        pltpu.make_async_copy(w_down, wd, w_sem.at[2]),
    ]

    barrier = pltpu.get_barrier_semaphore()
    for k in range(1, ctx_count):
        pl.semaphore_signal(barrier, inc=1, device_id=ctx_peer(k), device_id_type=MESH)
    for k in range(1, exp_count):
        pl.semaphore_signal(barrier, inc=1, device_id=exp_peer(k), device_id_type=MESH)
    pl.semaphore_wait(barrier, ctx_count + exp_count - 2)

    def piece_of(p, c, first):
        return page.at[pl.ds(c * chunk, chunk)] if first else kv.at[p, c]

    def right_copy(p, c, first=False):
        return remote(piece_of(p, c, first), kv.at[p, c], kv_right.at[p, c], kv_recv.at[p, c], {"ctx": ci + 1})

    def left_copy(p, c, first=False):
        return remote(piece_of(p, c, first), kv.at[p, c], kv_left.at[p, c], kv_recv.at[p, c], {"ctx": ci - 1})

    for c in range(chunks):
        @pl.when(ci < ctx_count - 1)
        def _():
            right_copy(ci, c, True).start()

        @pl.when(ci > 0)
        def _():
            left_copy(ci, c, True).start()

    own_page = [
        pltpu.make_async_copy(page.at[pl.ds(c * chunk, chunk)], kv.at[ci, c], kv_recv.at[ci, c])
        for c in range(chunks)
    ]
    for c in own_page:
        c.start()

    small = []
    for k in range(1, ctx_count):
        small.append(remote(ids, ids_all.at[k], ids_s.at[k], ids_r.at[k], ctx_peer(k)))
        small.append(remote(scores, scores_all.at[k], sc_s.at[k], sc_r.at[k], ctx_peer(k)))
    for c in small:
        c.start()
    for c in copies_w:
        c.start()

    for h in range(heads):
        q_rows[h * fresh:(h + 1) * fresh, :] = query[:, h * HEAD:(h + 1) * HEAD]
    accum[...] = jnp.zeros_like(accum)
    total[...] = jnp.zeros_like(total)
    peak[...] = jnp.full_like(peak, floor_value)

    step_rows = lax.broadcasted_iota(jnp.int32, (fresh, chunk), 1)
    position = lax.broadcasted_iota(jnp.int32, (fresh, chunk), 0) + ci * fresh

    def mask(p, c):
        offset = step_rows + c * chunk
        cached = (offset < slab) & (offset < lengths[p])
        new = (offset >= slab) & (p * fresh + offset - slab <= position)
        bias[...] = jnp.where(cached | new, 0.0, floor_value)

    def attend(source):
        both = source[...]
        keys = both[:, 0, :]
        values = both[:, 1, :]
        step = 2 if heads % 2 == 0 else 1
        for h in range(0, heads, step):
            sl = slice(h * fresh, (h + step) * fresh)
            s = lax.dot_general(
                q_rows[sl, :], keys, (((1,), (1,)), ((), ())), preferred_element_type=F32
            )
            s = jnp.concatenate([s[i * fresh:(i + 1) * fresh] + bias[...] for i in range(step)], 0)
            old = peak[sl, :]
            now = jnp.maximum(old, jnp.max(s, axis=1, keepdims=True))
            w = jnp.exp2((s - now[:, :1]) * scaling)
            fade = jnp.exp2((old - now) * scaling)
            total[sl, :] = total[sl, :] * fade + jnp.sum(w, axis=1, keepdims=True)
            accum[sl, :] = accum[sl, :] * fade + jnp.dot(
                w.astype(BF), values, preferred_element_type=F32
            )
            peak[sl, :] = now

    for c in range(chunks):
        own_page[c].wait()

    def own_chunk(c, carry):
        mask(ci, c)
        attend(kv.at[ci, c])
        return carry

    lax.fori_loop(0, chunks, own_chunk, 0)

    copies_w[1].wait()
    depth = 256

    def unpack(i, carry):
        at = pl.ds(pl.multiple_of(i * depth, depth), depth)
        block = wi[at]
        wg[at, :] = block[:, 0, :]
        wu[at, :] = block[:, 1, :]
        return carry

    lax.fori_loop(0, width // depth, unpack, 0)

    combined = scores[...] / jnp.sum(scores[...], axis=0, keepdims=True)
    ids_all[0] = ids[...]
    combine_all[0] = combined.astype(BF).astype(F32)
    for c in small:
        c.wait()
    for k in range(1, ctx_count):
        given = scores_all[k]
        combine_all[k] = (given / jnp.sum(given, axis=0, keepdims=True)).astype(BF).astype(F32)

    lanes = exp_count * capacity
    lane = lax.broadcasted_iota(jnp.int32, (lanes, rows), 0)
    wanted = ci * exp_count + lax.rem(ei + lane // capacity, exp_count)
    seat = (lane - lane // capacity * capacity).astype(F32)
    earlier = (
        lax.broadcasted_iota(jnp.int32, (rows, rows), 0)
        < lax.broadcasted_iota(jnp.int32, (rows, rows), 1)
    ).astype(F32)
    for k in range(ctx_count):
        chosen = jnp.zeros((lanes, rows), F32)
        portion = jnp.zeros((lanes, rows), F32)
        for j in range(top):
            hit = ids_all[k, j:j + 1, :] == wanted
            chosen = jnp.where(hit, 1.0, chosen)
            portion = jnp.where(hit, combine_all[k, j:j + 1, :], portion)
        rank = jnp.dot(chosen.astype(BF), earlier.astype(BF), preferred_element_type=F32)
        seated = (chosen > 0.5) & (rank == seat)
        place[k] = jnp.where(seated, 1.0, 0.0)
        gather[k] = jnp.where(seated, portion, 0.0)

    def arrival(i, carry):
        d = i // (2 * chunks) + 1
        c = lax.rem(i // 2, chunks)
        p = jnp.where(lax.rem(i, 2) == 0, ci - d, ci + d)

        @pl.when((p >= 0) & (p < ctx_count))
        def _():
            mask(p, c)
            right_copy(p, c).wait_recv()

            @pl.when((p < ci) & (ci < ctx_count - 1))
            def _():
                right_copy(p, c).start()

            @pl.when((p > ci) & (ci > 0))
            def _():
                left_copy(p, c).start()

            attend(kv.at[p, c])

        return carry

    lax.fori_loop(0, 2 * (ctx_count - 1) * chunks, arrival, 0)

    for h in range(heads):
        sl = slice(h * fresh, (h + 1) * fresh)
        context_out[:, h * HEAD:(h + 1) * HEAD] = (accum[sl, :] / total[sl, :]).astype(BF)

    copies_w[0].wait()

    pieces = 4
    piece = width // pieces
    own_share = []
    rs_copies = []
    for n in range(pieces):
        cols = slice(n * piece, (n + 1) * piece)
        part = jnp.dot(context_out[...], wo[:, cols], preferred_element_type=F32)
        rs_full[n] = part
        for k in range(1, exp_count):
            at = pl.ds(pl.multiple_of(lax.rem(ei + k, exp_count) * rows, rows), rows)
            rs_send[k, n] = rs_full[n, at, :].astype(BF)
            c = remote(rs_send.at[k, n], rs_recv.at[k, n], rs_s.at[k, n], rs_r.at[k, n], exp_peer(k))
            c.start()
            rs_copies.append(c)
    mine = pl.ds(pl.multiple_of(ei * rows, rows), rows)
    square = jnp.zeros((rows, 1), F32)
    for n in range(pieces):
        cols = slice(n * piece, (n + 1) * piece)
        share = rs_full[n, mine, :]
        for k in range(1, exp_count):
            rs_copies[n * (exp_count - 1) + k - 1].wait_recv()
            share = share + rs_recv[k, n].astype(F32)
        h = (residual[:, cols].astype(F32) + share).astype(BF)
        hidden[:, cols] = h
        wide = h.astype(F32)
        square = square + jnp.sum(wide * wide, axis=1, keepdims=True)
    inverse = lax.rsqrt(square / width + norm_epsilon)
    nz[0] = (hidden[...].astype(F32) * inverse * gain[...]).astype(BF)

    nz_copies = {}
    order = [1, ctx_count - 1] + list(range(2, ctx_count - 1)) if ctx_count > 2 else list(range(1, ctx_count))
    for k in reversed(order):
        c = remote(nz.at[0], nz.at[k], nz_s.at[k], nz_r.at[k], ctx_peer(k))
        c.start()
        nz_copies[k] = c

    dx_copies = []
    ret_copies = []
    mix_copies = {}
    own = None
    places = [0] + order
    half = (ctx_count + 1) // 2
    stages = [g for g in (places[:half], places[half:]) if g]

    def dispatch(k):
        if k:
            nz_copies[k].wait_recv()
        routed = jnp.dot(place[k].astype(BF), nz[k], preferred_element_type=F32)
        for j in range(exp_count):
            block = routed[j * capacity:(j + 1) * capacity].astype(BF)
            if j == 0:
                x_recv[0, k] = block
            else:
                x_send[j, k] = block
                c = remote(x_send.at[j, k], x_recv.at[j, k], dx_s.at[j, k], dx_r.at[j, k], exp_peer(j))
                c.start()
                dx_copies.append(c)

    def experts(group):
        for k in group:
            for j in range(1, exp_count):
                dx_copies[places.index(k) * (exp_count - 1) + j - 1].wait_recv()
        count = len(group) * exp_count * capacity
        for j in range(exp_count):
            for n, k in enumerate(group):
                at = slice((j * len(group) + n) * capacity, (j * len(group) + n + 1) * capacity)
                x_rows[at, :] = x_recv[j, k].astype(F32)
        x = x_rows[:count, :].astype(BF)
        gate = jnp.dot(x, wg[...], preferred_element_type=F32)
        up = jnp.dot(x, wu[...], preferred_element_type=F32)
        act = (gate / (1.0 + jnp.exp(-gate)) * up).astype(BF)
        result = jnp.dot(act, wd[...], preferred_element_type=F32)
        for n, k in enumerate(group):
            for j in range(exp_count):
                first = (j * len(group) + n) * capacity
                block = result[first:first + capacity].astype(BF)
                if j == 0:
                    y_recv[0, k] = block
                else:
                    y_send[j, k] = block
                    c = remote(y_send.at[j, k], y_recv.at[j, k], ret_s.at[j, k], ret_r.at[j, k], exp_peer(exp_count - j))
                    c.start()
                    ret_copies.append(c)

    def mixing(k):
        for j in range(1, exp_count):
            ret_copies[places.index(k) * (exp_count - 1) + j - 1].wait_recv()
        rows_k = jnp.concatenate([y_recv[j, k].astype(F32) for j in range(exp_count)], 0).astype(BF)
        mixed = lax.dot_general(
            gather[k].astype(BF), rows_k, (((0,), (0,)), ((), ())), preferred_element_type=F32
        )
        if k == 0:
            return mixed
        mix_send[k] = mixed.astype(BF)
        c = remote(mix_send.at[k], mix_recv.at[k], mix_s.at[k], mix_r.at[k], ctx_peer(ctx_count - k))
        c.start()
        mix_copies[k] = c

    for k in stages[0]:
        dispatch(k)
    copies_w[2].wait()
    experts(stages[0])
    for group in stages[1:]:
        for k in group:
            dispatch(k)
        experts(group)
    for k in places[1:]:
        mixing(k)
    own = mixing(0)
    out = hidden[...].astype(F32) + own
    for k in order:
        mix_copies[k].wait_recv()
        out = out + mix_recv[k].astype(F32)
    layer_out[...] = out.astype(BF)

    for c in rs_copies + list(nz_copies.values()) + dx_copies + ret_copies + list(mix_copies.values()):
        c.wait_send()

    for c in range(chunks):
        @pl.when(ci < ctx_count - 1)
        def _():
            right_copy(ci, c, True).wait_send()

        @pl.when(ci > 0)
        def _():
            left_copy(ci, c, True).wait_send()

    def drain(i, carry):
        p = i // chunks
        c = lax.rem(i, chunks)

        @pl.when((p < ci) & (ci < ctx_count - 1))
        def _():
            right_copy(p, c).wait_send()

        @pl.when((p > ci) & (ci > 0))
        def _():
            left_copy(p, c).wait_send()

        return carry

    lax.fori_loop(0, ctx_count * chunks, drain, 0)


def settle(context, layer, context_out, layer_out):
    context_out[...] = context[...]
    layer_out[...] = layer[...]


def fused_device(
    ctx_count, exp_count, queries, pages, cached_lengths, residual_in, out_weight, norm_gain,
    expert_ids, route_scores, expert_input, expert_output,
):
    fresh, query_width = queries.shape[1:]
    page_size = pages.shape[1]
    rows, width = residual_in.shape[1:]
    top = expert_ids.shape[2]
    hidden_width = expert_input.shape[3]
    experts = ctx_count * exp_count
    capacity = max(2, -(-rows * top // experts))
    stacked = query_width // HEAD * fresh
    span = ctx_count * capacity
    vm = pl.BlockSpec(memory_space=pltpu.VMEM)
    sm = pl.BlockSpec(memory_space=pltpu.SMEM)
    hbm = pl.BlockSpec(memory_space=pl.ANY)
    dma = pltpu.SemaphoreType.DMA
    V = pltpu.VMEM
    lanes = exp_count * capacity
    pieces = 4
    chunks = next(n for n in (3, 2, 1) if page_size % (16 * n) == 0 or n == 1)
    context, layer_out = pl.pallas_call(
        functools.partial(fused_kernel, ctx_count, exp_count, capacity),
        out_shape=(
            jax.ShapeDtypeStruct((fresh, query_width), BF),
            jax.ShapeDtypeStruct((rows, width), BF),
        ),
        in_specs=[sm, vm, hbm, vm, vm, vm, vm, hbm, hbm, hbm],
        out_specs=(vm, vm),
        scratch_shapes=[
            V((ctx_count, chunks, page_size // chunks) + pages.shape[2:], BF),
            V((stacked, HEAD), BF),
            V((fresh, page_size // chunks), F32),
            V((stacked, HEAD), F32),
            V((stacked, HEAD), F32),
            V((stacked, HEAD), F32),
            V(out_weight.shape, BF),
            V(expert_input.shape[1:], BF),
            V((width, hidden_width), BF),
            V((width, hidden_width), BF),
            V(expert_output.shape[1:], BF),
            V((ctx_count, top, rows), jnp.int32),
            V((ctx_count, top, rows), F32),
            V((ctx_count, top, rows), F32),
            V((ctx_count, lanes, rows), F32),
            V((ctx_count, lanes, rows), F32),
            V((pieces, fresh, width // pieces), F32),
            V((exp_count, pieces, rows, width // pieces), BF),
            V((exp_count, pieces, rows, width // pieces), BF),
            V((rows, width), BF),
            V((ctx_count, rows, width), BF),
            V((exp_count, ctx_count, capacity, width), BF),
            V((exp_count, ctx_count, capacity, width), BF),
            V((exp_count * span, width), F32),
            V((exp_count, ctx_count, capacity, width), BF),
            V((exp_count, ctx_count, capacity, width), BF),
            V((ctx_count, rows, width), BF),
            V((ctx_count, rows, width), BF),
            dma((ctx_count, chunks)), dma((ctx_count, chunks)), dma((ctx_count, chunks)), dma((3,)),
            dma((ctx_count,)), dma((ctx_count,)), dma((ctx_count,)), dma((ctx_count,)),
            dma((exp_count, pieces)), dma((exp_count, pieces)),
            dma((ctx_count,)), dma((ctx_count,)),
            dma((exp_count, ctx_count)), dma((exp_count, ctx_count)),
            dma((exp_count, ctx_count)), dma((exp_count, ctx_count)),
            dma((ctx_count,)), dma((ctx_count,)),
        ],
        compiler_params=pltpu.CompilerParams(
            collective_id=0, has_side_effects=True, vmem_limit_bytes=VMEM_LIMIT
        ),
    )(
        cached_lengths[0], queries[0], pages[0], residual_in[0], norm_gain.reshape(1, width),
        expert_ids[0].T, route_scores[0].T, out_weight, expert_input[0], expert_output[0],
    )
    context, layer_out = pl.pallas_call(
        settle,
        out_shape=(
            jax.ShapeDtypeStruct(context.shape, BF),
            jax.ShapeDtypeStruct(layer_out.shape, BF),
        ),
        in_specs=[vm, vm],
        out_specs=(vm, vm),
    )(context, layer_out)
    return context[None], layer_out[None]


def fused_fits(mesh):
    return mesh.shape["rep"] == 1 and mesh.shape["ctx"] <= 8


def solution(mesh):
    in_specs = (
        P("groups", "ctx", ("exp", "rep")),
        P("groups", "ctx", None, "exp"),
        P("groups", None),
        P("groups", ("ctx", "exp"), None),
        P(("exp", "rep"), None),
        P(),
        P("groups", ("ctx", "exp"), None),
        P("groups", ("ctx", "exp"), None),
        P(("ctx", "exp"), None, None, "rep"),
        P(("ctx", "exp"), "rep", None),
    )
    out_specs = (P("groups", "ctx", ("exp", "rep")), P("groups", ("ctx", "exp", "rep"), None))
    body = per_device
    if fused_fits(mesh):
        body = functools.partial(fused_device, mesh.shape["ctx"], mesh.shape["exp"])
    return jax.shard_map(
        body, mesh=mesh, in_specs=in_specs, out_specs=out_specs, check_vma=False
    )
```

```python
import functools

import jax
import jax.numpy as jnp
from jax import lax
from jax.experimental import pallas as pl
from jax.experimental.pallas import tpu as pltpu
from jax.sharding import PartitionSpec as P

HEAD = 128


floor_value = -1e30
norm_epsilon = 1e-06


def normalize(hidden, norm_gain):
    widened = hidden.astype(jnp.float32)
    mean_square = jnp.mean(widened * widened, axis=-1, keepdims=True)
    return (widened * lax.rsqrt(mean_square + norm_epsilon) * norm_gain).astype(jnp.bfloat16)


def attend_piece(query_rows, page_rows, allowed):
    scaling = query_rows.shape[-1] ** (-0.5)
    scores = (
        jnp.einsum(
            "rqhe,rke->rqhk", query_rows, page_rows[:, :, 0], preferred_element_type=jnp.float32
        )
        * scaling
    )
    permitted = allowed[:, :, None, :]
    masked = jnp.where(permitted, scores, floor_value)
    peaks = jnp.max(masked, axis=-1)
    weights = jnp.where(permitted, jnp.exp(masked - peaks[..., None]), 0.0)
    totals = jnp.sum(weights, axis=-1)
    summed = jnp.einsum(
        "rqhk,rke->rqhe",
        weights.astype(jnp.bfloat16),
        page_rows[:, :, 1],
        preferred_element_type=jnp.float32,
    )
    return (peaks, totals, summed)


def merge_partials(earlier, later):
    peaks = jnp.maximum(earlier[0], later[0])
    later_scale = jnp.exp(later[0] - peaks)
    totals = later[1] * later_scale
    summed = later[2] * later_scale[..., None]
    return (peaks, totals, summed)


def rows_mask(row_index, lengths, query_positions, slab_size, fresh_block):
    page_size = slab_size + fresh_block
    page_number = row_index // page_size
    offset = row_index - page_number * page_size
    page_count = lengths.shape[1]
    picker = page_number[None, :] == jnp.arange(page_count, dtype=jnp.int32)[:, None]
    live_length = jnp.sum(jnp.where(picker[None], lengths[:, :, None], 0), axis=1)
    in_cache = (offset < slab_size)[None, :] & (offset[None, :] < live_length)
    fresh_position = page_number * fresh_block + offset - slab_size
    in_fresh = (offset >= slab_size)[None, :] & (
        fresh_position[None, :] <= query_positions[:, None]
    )
    return in_cache[:, None, :] | in_fresh[None, :, :]


def per_device(
    queries,
    pages,
    cached_lengths,
    residual_in,
    out_weight,
    norm_gain,
    expert_ids,
    route_scores,
    expert_input,
    expert_output,
):
    requests, fresh_block, query_width = queries.shape
    local_heads = query_width // HEAD
    core_place = lax.axis_index("rep")
    page_place = lax.axis_index("ctx")
    rep_count = lax.axis_size("rep")
    page_size = pages.shape[1]
    slab_size = page_size - fresh_block
    own_positions = page_place * fresh_block + jnp.arange(fresh_block, dtype=jnp.int32)
    query_rows = queries.reshape(requests, fresh_block, local_heads, HEAD)
    start_state = (
        jnp.full((requests, fresh_block, local_heads), floor_value, jnp.float32),
        jnp.zeros((requests, fresh_block, local_heads), jnp.float32),
        jnp.zeros((requests, fresh_block, local_heads, HEAD), jnp.float32),
    )
    page_piece = lax.all_gather(pages, "ctx", axis=1, tiled=True)
    row_index = jnp.arange(page_piece.shape[1], dtype=jnp.int32)
    allowed = rows_mask(row_index, cached_lengths, own_positions, slab_size, fresh_block)
    peaks, totals, summed = merge_partials(
        start_state, attend_piece(query_rows, page_piece, allowed)
    )
    context = (
        (summed / totals[..., None])
        .astype(jnp.bfloat16)
        .reshape(requests, fresh_block, query_width)
    )
    projected = jnp.dot(
        context.reshape(requests * fresh_block, query_width),
        out_weight,
        preferred_element_type=jnp.float32,
    ).reshape(requests, fresh_block, -1)
    token_block = residual_in.shape[1]
    share_size = token_block // rep_count
    own_share = lax.psum_scatter(
        projected.astype(jnp.bfloat16), ("exp", "rep"), scatter_dimension=1, tiled=True
    ).astype(jnp.float32)
    own_residual = lax.dynamic_slice_in_dim(residual_in, core_place * share_size, share_size, 1)
    own_hidden = (own_residual.astype(jnp.float32) + own_share).astype(jnp.bfloat16)
    normed = lax.all_gather(normalize(own_hidden, norm_gain), "rep", axis=1, tiled=True)
    top_count = expert_ids.shape[2]
    expert_count = lax.axis_size("ctx") * lax.axis_size("exp")
    most_rows = max(2, (token_block * top_count + expert_count - 1) // expert_count)
    capacity = requests * most_rows
    model_width = normed.shape[2]
    token_count = requests * token_block
    flat_ids = expert_ids.reshape(-1)
    row_count = flat_ids.shape[0]
    chosen = (flat_ids[:, None] == jnp.arange(expert_count, dtype=jnp.int32)[None, :]).astype(
        jnp.int32
    )
    earlier_rows = jnp.cumsum(chosen, axis=0) - chosen
    slot_rank = jnp.sum(earlier_rows * chosen, axis=1)
    slot_index = flat_ids * capacity + slot_rank
    slot_onehot = (
        slot_index[:, None] == jnp.arange(expert_count * capacity, dtype=jnp.int32)[None, :]
    ).astype(jnp.bfloat16)
    token_onehot = (
        (jnp.arange(row_count, dtype=jnp.int32) // top_count)[:, None]
        == jnp.arange(token_count, dtype=jnp.int32)[None, :]
    ).astype(jnp.bfloat16)
    placement = jnp.dot(slot_onehot.T, token_onehot, preferred_element_type=jnp.float32).astype(
        jnp.bfloat16
    )
    outgoing = jnp.dot(
        placement, normed.reshape(token_count, model_width), preferred_element_type=jnp.float32
    )
    outgoing = outgoing.astype(jnp.bfloat16).reshape(expert_count, capacity, model_width)
    scores_sum = jnp.sum(route_scores, axis=2, keepdims=True)
    combine = (route_scores / scores_sum).astype(jnp.bfloat16).reshape(-1)
    gathering = jnp.dot(
        (token_onehot * combine[:, None]).T, slot_onehot, preferred_element_type=jnp.float32
    ).astype(jnp.bfloat16)
    gate_up = expert_input[0]
    down_weight = expert_output[0]
    arrived_rows = lax.all_to_all(outgoing, ("ctx", "exp"), split_axis=0, concat_axis=0, tiled=True)
    inner_rows = jnp.einsum(
        "nd,dgh->ngh",
        arrived_rows.reshape(-1, model_width),
        gate_up,
        preferred_element_type=jnp.float32,
    )
    activated = (jax.nn.silu(inner_rows[:, 0]) * inner_rows[:, 1]).astype(jnp.bfloat16)
    result = jnp.dot(activated, down_weight, preferred_element_type=jnp.float32).astype(
        jnp.bfloat16
    )
    returned = lax.all_to_all(
        result.reshape(arrived_rows.shape), ("ctx", "exp"), split_axis=0, concat_axis=0, tiled=True
    )
    mixture = jnp.dot(
        gathering,
        returned.reshape(expert_count * capacity, model_width),
        preferred_element_type=jnp.float32,
    )
    own_mixture = lax.psum_scatter(
        mixture.reshape(requests, token_block, model_width).astype(jnp.bfloat16),
        "rep",
        scatter_dimension=1,
        tiled=True,
    ).astype(jnp.float32)
    layer_out = (own_hidden.astype(jnp.float32) + own_mixture).astype(jnp.bfloat16)
    return (context, layer_out)


BF = jnp.bfloat16
F32 = jnp.float32
MESH = pl.DeviceIdType.MESH
VMEM_LIMIT = 60 * 1024 * 1024


def fused_kernel(
    ctx_count, exp_count, capacity,
    lengths, query, page, residual, gain, ids, scores, w_out, w_in, w_down,
    context_out, layer_out,
    kv, raw, q_rows, bias, peak, total, accum, wo, wi, wg, wu, wd,
    ids_all, scores_all, combine_all, place, gather,
    rs_full, rs_send, rs_recv, hidden, nz, x_send, x_recv, x_rows, y_send, y_recv, mix_send, mix_recv,
    kv_left, kv_right, kv_recv, w_sem,
    ids_s, ids_r, sc_s, sc_r, rs_s, rs_r, nz_s, nz_r, dx_s, dx_r, ret_s, ret_r, mix_s, mix_r,
):
    ci = lax.axis_index("ctx")
    ei = lax.axis_index("exp")
    fresh = query.shape[0]
    heads = query.shape[1] // HEAD
    page_size = page.shape[0]
    slab = page_size - fresh
    rows = residual.shape[0]
    width = residual.shape[1]
    top = ids.shape[0]
    chunks = kv.shape[1]
    chunk = kv.shape[2]
    scaling = HEAD ** (-0.5) * 1.4426950408889634

    def ctx_peer(k):
        return {"ctx": lax.rem(ci + k, ctx_count)}

    def exp_peer(k):
        return {"exp": lax.rem(ei + k, exp_count)}

    def remote(src, dst, ss, rs, where):
        return pltpu.make_async_remote_copy(
            src_ref=src, dst_ref=dst, send_sem=ss, recv_sem=rs, device_id=where, device_id_type=MESH
        )

    copies_w = [
        pltpu.make_async_copy(w_out, wo, w_sem.at[0]),
        pltpu.make_async_copy(w_in, wi, w_sem.at[1]),
        pltpu.make_async_copy(w_down, wd, w_sem.at[2]),
    ]

    own_page = [
        pltpu.make_async_copy(page.at[pl.ds(c * chunk, chunk)], raw.at[c], kv_recv.at[ci, c])
        for c in range(chunks)
    ]
    for c in own_page:
        c.start()

    barrier = pltpu.get_barrier_semaphore()
    for k in range(1, ctx_count):
        pl.semaphore_signal(barrier, inc=1, device_id=ctx_peer(k), device_id_type=MESH)
    for k in range(1, exp_count):
        pl.semaphore_signal(barrier, inc=1, device_id=exp_peer(k), device_id_type=MESH)
    for c in range(chunks):
        own_page[c].wait()
        both = raw[c]
        kv[ci, c, :, :HEAD] = both[:, 0, :]
        kv[ci, c, :, HEAD:] = both[:, 1, :]
    pl.semaphore_wait(barrier, ctx_count + exp_count - 2)

    def right_copy(p, c):
        return remote(kv.at[p, c], kv.at[p, c], kv_right.at[p, c], kv_recv.at[p, c], {"ctx": ci + 1})

    def left_copy(p, c):
        return remote(kv.at[p, c], kv.at[p, c], kv_left.at[p, c], kv_recv.at[p, c], {"ctx": ci - 1})

    for c in range(chunks):
        @pl.when(ci < ctx_count - 1)
        def _():
            right_copy(ci, c).start()

        @pl.when(ci > 0)
        def _():
            left_copy(ci, c).start()

    small = []
    for k in range(1, ctx_count):
        small.append(remote(ids, ids_all.at[k], ids_s.at[k], ids_r.at[k], ctx_peer(k)))
        small.append(remote(scores, scores_all.at[k], sc_s.at[k], sc_r.at[k], ctx_peer(k)))
    for c in small:
        c.start()
    for c in copies_w:
        c.start()

    for h in range(heads):
        q_rows[h * fresh:(h + 1) * fresh, :] = query[:, h * HEAD:(h + 1) * HEAD]
    accum[...] = jnp.zeros_like(accum)
    total[...] = jnp.zeros_like(total)
    peak[...] = jnp.full_like(peak, floor_value)

    step_rows = lax.broadcasted_iota(jnp.int32, (fresh, chunk), 1)
    position = lax.broadcasted_iota(jnp.int32, (fresh, chunk), 0) + ci * fresh

    def mask(p, c):
        offset = step_rows + c * chunk
        cached = (offset < slab) & (offset < lengths[p])
        new = (offset >= slab) & (p * fresh + offset - slab <= position)
        bias[...] = jnp.where(cached | new, 0.0, floor_value)

    def attend(source):
        keys = source[:, :HEAD]
        values = source[:, HEAD:]
        step = 2 if heads % 2 == 0 else 1
        for h in range(0, heads, step):
            sl = slice(h * fresh, (h + step) * fresh)
            s = lax.dot_general(
                q_rows[sl, :], keys, (((1,), (1,)), ((), ())), preferred_element_type=F32
            )
            s = jnp.concatenate([s[i * fresh:(i + 1) * fresh] + bias[...] for i in range(step)], 0)
            old = peak[sl, :]
            now = jnp.maximum(old, jnp.max(s, axis=1, keepdims=True))
            w = jnp.exp2((s - now[:, :1]) * scaling)
            fade = jnp.exp2((old - now) * scaling)
            total[sl, :] = total[sl, :] * fade + jnp.sum(w, axis=1, keepdims=True)
            accum[sl, :] = accum[sl, :] * fade + jnp.dot(
                w.astype(BF), values, preferred_element_type=F32
            )
            peak[sl, :] = now

    def own_chunk(c, carry):
        mask(ci, c)
        attend(kv.at[ci, c])
        return carry

    lax.fori_loop(0, chunks, own_chunk, 0)

    copies_w[1].wait()
    depth = 256

    def unpack(i, carry):
        at = pl.ds(pl.multiple_of(i * depth, depth), depth)
        block = wi[at]
        wg[at, :] = block[:, 0, :]
        wu[at, :] = block[:, 1, :]
        return carry

    lax.fori_loop(0, width // depth, unpack, 0)

    combined = scores[...] / jnp.sum(scores[...], axis=0, keepdims=True)
    ids_all[0] = ids[...]
    combine_all[0] = combined.astype(BF).astype(F32)
    for c in small:
        c.wait()
    for k in range(1, ctx_count):
        given = scores_all[k]
        combine_all[k] = (given / jnp.sum(given, axis=0, keepdims=True)).astype(BF).astype(F32)

    lanes = exp_count * capacity
    lane = lax.broadcasted_iota(jnp.int32, (lanes, rows), 0)
    wanted = ci * exp_count + lax.rem(ei + lane // capacity, exp_count)
    seat = (lane - lane // capacity * capacity).astype(F32)
    earlier = (
        lax.broadcasted_iota(jnp.int32, (rows, rows), 0)
        < lax.broadcasted_iota(jnp.int32, (rows, rows), 1)
    ).astype(F32)
    for k in range(ctx_count):
        chosen = jnp.zeros((lanes, rows), F32)
        portion = jnp.zeros((lanes, rows), F32)
        for j in range(top):
            hit = ids_all[k, j:j + 1, :] == wanted
            chosen = jnp.where(hit, 1.0, chosen)
            portion = jnp.where(hit, combine_all[k, j:j + 1, :], portion)
        rank = jnp.dot(chosen.astype(BF), earlier.astype(BF), preferred_element_type=F32)
        seated = (chosen > 0.5) & (rank == seat)
        place[k] = jnp.where(seated, 1.0, 0.0)
        gather[k] = jnp.where(seated, portion, 0.0)

    def arrival(i, carry):
        d = i // (2 * chunks) + 1
        c = lax.rem(i // 2, chunks)
        p = jnp.where(lax.rem(i, 2) == 0, ci - d, ci + d)

        @pl.when((p >= 0) & (p < ctx_count))
        def _():
            mask(p, c)
            right_copy(p, c).wait_recv()

            @pl.when((p < ci) & (ci < ctx_count - 1))
            def _():
                right_copy(p, c).start()

            @pl.when((p > ci) & (ci > 0))
            def _():
                left_copy(p, c).start()

            attend(kv.at[p, c])

        return carry

    lax.fori_loop(0, 2 * (ctx_count - 1) * chunks, arrival, 0)

    for h in range(heads):
        sl = slice(h * fresh, (h + 1) * fresh)
        context_out[:, h * HEAD:(h + 1) * HEAD] = (accum[sl, :] / total[sl, :]).astype(BF)

    copies_w[0].wait()

    pieces = 4
    piece = width // pieces
    own_share = []
    rs_copies = []
    for n in range(pieces):
        cols = slice(n * piece, (n + 1) * piece)
        part = jnp.dot(context_out[...], wo[:, cols], preferred_element_type=F32)
        rs_full[n] = part
        for k in range(1, exp_count):
            at = pl.ds(pl.multiple_of(lax.rem(ei + k, exp_count) * rows, rows), rows)
            rs_send[k, n] = rs_full[n, at, :].astype(BF)
            c = remote(rs_send.at[k, n], rs_recv.at[k, n], rs_s.at[k, n], rs_r.at[k, n], exp_peer(k))
            c.start()
            rs_copies.append(c)
    mine = pl.ds(pl.multiple_of(ei * rows, rows), rows)
    square = jnp.zeros((rows, 1), F32)
    for n in range(pieces):
        cols = slice(n * piece, (n + 1) * piece)
        share = rs_full[n, mine, :]
        for k in range(1, exp_count):
            rs_copies[n * (exp_count - 1) + k - 1].wait_recv()
            share = share + rs_recv[k, n].astype(F32)
        h = (residual[:, cols].astype(F32) + share).astype(BF)
        hidden[:, cols] = h
        wide = h.astype(F32)
        square = square + jnp.sum(wide * wide, axis=1, keepdims=True)
    inverse = lax.rsqrt(square / width + norm_epsilon)
    nz[0] = (hidden[...].astype(F32) * inverse * gain[...]).astype(BF)

    nz_copies = {}
    order = [1, ctx_count - 1] + list(range(2, ctx_count - 1)) if ctx_count > 2 else list(range(1, ctx_count))
    for k in reversed(order):
        c = remote(nz.at[0], nz.at[k], nz_s.at[k], nz_r.at[k], ctx_peer(k))
        c.start()
        nz_copies[k] = c

    dx_copies = []
    ret_copies = []
    mix_copies = {}
    own = None
    places = [0] + order
    stages = [places]

    def dispatch(k):
        if k:
            nz_copies[k].wait_recv()
        routed = jnp.dot(place[k].astype(BF), nz[k], preferred_element_type=F32)
        for j in range(exp_count):
            block = routed[j * capacity:(j + 1) * capacity].astype(BF)
            if j == 0:
                x_recv[0, k] = block
            else:
                x_send[j, k] = block
                c = remote(x_send.at[j, k], x_recv.at[j, k], dx_s.at[j, k], dx_r.at[j, k], exp_peer(j))
                c.start()
                dx_copies.append(c)

    def experts(group):
        for k in group:
            for j in range(1, exp_count):
                dx_copies[places.index(k) * (exp_count - 1) + j - 1].wait_recv()
        count = len(group) * exp_count * capacity
        for j in range(exp_count):
            for n, k in enumerate(group):
                at = slice((j * len(group) + n) * capacity, (j * len(group) + n + 1) * capacity)
                x_rows[at, :] = x_recv[j, k].astype(F32)
        x = x_rows[:count, :].astype(BF)
        gate = jnp.dot(x, wg[...], preferred_element_type=F32)
        up = jnp.dot(x, wu[...], preferred_element_type=F32)
        act = (gate / (1.0 + jnp.exp(-gate)) * up).astype(BF)
        result = jnp.dot(act, wd[...], preferred_element_type=F32)
        for n, k in enumerate(group):
            for j in range(exp_count):
                first = (j * len(group) + n) * capacity
                block = result[first:first + capacity].astype(BF)
                if j == 0:
                    y_recv[0, k] = block
                else:
                    y_send[j, k] = block
                    c = remote(y_send.at[j, k], y_recv.at[j, k], ret_s.at[j, k], ret_r.at[j, k], exp_peer(exp_count - j))
                    c.start()
                    ret_copies.append(c)

    def mixing(k):
        for j in range(1, exp_count):
            ret_copies[places.index(k) * (exp_count - 1) + j - 1].wait_recv()
        rows_k = jnp.concatenate([y_recv[j, k].astype(F32) for j in range(exp_count)], 0).astype(BF)
        mixed = lax.dot_general(
            gather[k].astype(BF), rows_k, (((0,), (0,)), ((), ())), preferred_element_type=F32
        )
        if k == 0:
            return mixed
        mix_send[k] = mixed.astype(BF)
        c = remote(mix_send.at[k], mix_recv.at[k], mix_s.at[k], mix_r.at[k], ctx_peer(ctx_count - k))
        c.start()
        mix_copies[k] = c

    for k in stages[0]:
        dispatch(k)
    copies_w[2].wait()
    experts(stages[0])
    for group in stages[1:]:
        for k in group:
            dispatch(k)
        experts(group)
    for k in places[1:]:
        mixing(k)
    own = mixing(0)
    out = hidden[...].astype(F32) + own
    for k in order:
        mix_copies[k].wait_recv()
        out = out + mix_recv[k].astype(F32)
    layer_out[...] = out.astype(BF)

    for c in rs_copies + list(nz_copies.values()) + dx_copies + ret_copies + list(mix_copies.values()):
        c.wait_send()

    for c in range(chunks):
        @pl.when(ci < ctx_count - 1)
        def _():
            right_copy(ci, c).wait_send()

        @pl.when(ci > 0)
        def _():
            left_copy(ci, c).wait_send()

    def drain(i, carry):
        p = i // chunks
        c = lax.rem(i, chunks)

        @pl.when((p < ci) & (ci < ctx_count - 1))
        def _():
            right_copy(p, c).wait_send()

        @pl.when((p > ci) & (ci > 0))
        def _():
            left_copy(p, c).wait_send()

        return carry

    lax.fori_loop(0, ctx_count * chunks, drain, 0)


def settle(context, layer, context_out, layer_out):
    context_out[...] = context[...]
    layer_out[...] = layer[...]


def fused_device(
    ctx_count, exp_count, queries, pages, cached_lengths, residual_in, out_weight, norm_gain,
    expert_ids, route_scores, expert_input, expert_output,
):
    fresh, query_width = queries.shape[1:]
    page_size = pages.shape[1]
    rows, width = residual_in.shape[1:]
    top = expert_ids.shape[2]
    hidden_width = expert_input.shape[3]
    experts = ctx_count * exp_count
    capacity = max(2, -(-rows * top // experts))
    stacked = query_width // HEAD * fresh
    span = ctx_count * capacity
    vm = pl.BlockSpec(memory_space=pltpu.VMEM)
    sm = pl.BlockSpec(memory_space=pltpu.SMEM)
    hbm = pl.BlockSpec(memory_space=pl.ANY)
    dma = pltpu.SemaphoreType.DMA
    V = pltpu.VMEM
    lanes = exp_count * capacity
    pieces = 4
    chunks = next(n for n in (3, 2, 1) if page_size % (16 * n) == 0 or n == 1)
    context, layer_out = pl.pallas_call(
        functools.partial(fused_kernel, ctx_count, exp_count, capacity),
        out_shape=(
            jax.ShapeDtypeStruct((fresh, query_width), BF),
            jax.ShapeDtypeStruct((rows, width), BF),
        ),
        in_specs=[sm, vm, hbm, vm, vm, vm, vm, hbm, hbm, hbm],
        out_specs=(vm, vm),
        scratch_shapes=[
            V((ctx_count, chunks, page_size // chunks, 2 * HEAD), BF),
            V((chunks, page_size // chunks) + pages.shape[2:], BF),
            V((stacked, HEAD), BF),
            V((fresh, page_size // chunks), F32),
            V((stacked, HEAD), F32),
            V((stacked, HEAD), F32),
            V((stacked, HEAD), F32),
            V(out_weight.shape, BF),
            V(expert_input.shape[1:], BF),
            V((width, hidden_width), BF),
            V((width, hidden_width), BF),
            V(expert_output.shape[1:], BF),
            V((ctx_count, top, rows), jnp.int32),
            V((ctx_count, top, rows), F32),
            V((ctx_count, top, rows), F32),
            V((ctx_count, lanes, rows), F32),
            V((ctx_count, lanes, rows), F32),
            V((pieces, fresh, width // pieces), F32),
            V((exp_count, pieces, rows, width // pieces), BF),
            V((exp_count, pieces, rows, width // pieces), BF),
            V((rows, width), BF),
            V((ctx_count, rows, width), BF),
            V((exp_count, ctx_count, capacity, width), BF),
            V((exp_count, ctx_count, capacity, width), BF),
            V((exp_count * span, width), F32),
            V((exp_count, ctx_count, capacity, width), BF),
            V((exp_count, ctx_count, capacity, width), BF),
            V((ctx_count, rows, width), BF),
            V((ctx_count, rows, width), BF),
            dma((ctx_count, chunks)), dma((ctx_count, chunks)), dma((ctx_count, chunks)), dma((3,)),
            dma((ctx_count,)), dma((ctx_count,)), dma((ctx_count,)), dma((ctx_count,)),
            dma((exp_count, pieces)), dma((exp_count, pieces)),
            dma((ctx_count,)), dma((ctx_count,)),
            dma((exp_count, ctx_count)), dma((exp_count, ctx_count)),
            dma((exp_count, ctx_count)), dma((exp_count, ctx_count)),
            dma((ctx_count,)), dma((ctx_count,)),
        ],
        compiler_params=pltpu.CompilerParams(
            collective_id=0, has_side_effects=True, vmem_limit_bytes=VMEM_LIMIT
        ),
    )(
        cached_lengths[0], queries[0], pages[0], residual_in[0], norm_gain.reshape(1, width),
        expert_ids[0].T, route_scores[0].T, out_weight, expert_input[0], expert_output[0],
    )
    context, layer_out = pl.pallas_call(
        settle,
        out_shape=(
            jax.ShapeDtypeStruct(context.shape, BF),
            jax.ShapeDtypeStruct(layer_out.shape, BF),
        ),
        in_specs=[vm, vm],
        out_specs=(vm, vm),
    )(context, layer_out)
    return context[None], layer_out[None]


def fused_fits(mesh):
    return mesh.shape["rep"] == 1 and mesh.shape["ctx"] <= 8


def solution(mesh):
    in_specs = (
        P("groups", "ctx", ("exp", "rep")),
        P("groups", "ctx", None, "exp"),
        P("groups", None),
        P("groups", ("ctx", "exp"), None),
        P(("exp", "rep"), None),
        P(),
        P("groups", ("ctx", "exp"), None),
        P("groups", ("ctx", "exp"), None),
        P(("ctx", "exp"), None, None, "rep"),
        P(("ctx", "exp"), "rep", None),
    )
    out_specs = (P("groups", "ctx", ("exp", "rep")), P("groups", ("ctx", "exp", "rep"), None))
    body = per_device
    if fused_fits(mesh):
        body = functools.partial(fused_device, mesh.shape["ctx"], mesh.shape["exp"])
    return jax.shard_map(
        body, mesh=mesh, in_specs=in_specs, out_specs=out_specs, check_vma=False
    )
```
